32 devices in a mesh: frame: 4 (over z), pipe: 4 (over x, core), dp: 2 (over y).
Axes of the slice: x: 2, y: 2, z: 4, core: 2. Of those that a mesh axis runs over, the one named last changes fastest.
Arguments:
- acts: bfloat16 [4, 2, 32, 4, 1280], P('pipe', 'dp', 'frame'), may hold values from -18 to 18
- cotangent: bfloat16 [4, 2, 32, 4, 1280], P('pipe', 'dp', 'frame'), may hold values from -6 to 6
- w_query: bfloat16 [4, 1280, 768], P('pipe'), may hold values from -0.15625 to 0.15625
- w_key: bfloat16 [4, 1280, 768], P('pipe'), may hold values from -0.15625 to 0.15625
- w_value: bfloat16 [4, 1280, 768], P('pipe'), may hold values from -0.15625 to 0.15625
- w_out: bfloat16 [4, 1280, 768], P('pipe'), may hold values from -0.21875 to 0.21875
Outputs:
- sent_grad: bfloat16 [4, 2, 32, 4, 1280], P('pipe', 'dp', 'frame')
- grad_value: float32 [4, 1280, 768], P('pipe', None, ('frame', 'dp'))
The draws below stay inside these ranges and needn't reach their ends.
All inputs are finite; a program needn't handle non-finite values.
Results may differ from the reference program's by a relative error of at most 0.017.
The reference program's roundings to bfloat16 on the way count: a program that leaves them out, or rounds other values in their place, can miss the bound.
Values may be sent and summed in bfloat16 or wider, within the bound.
No kernel may reach another device: no remote copies, remote signals or barrier semaphores. Data moves between devices by JAX's collectives and lax.ppermute only.
A program may use at most 64 MiB of HBM per device.

```python
import jax
import jax.numpy as jnp
from jax import lax

C = 1280
HEADS = 12
HEAD_DIM = 64
INNER = 768
FRAMES = 32
POS = 4
CLIPS = 2
PIPE = 4


def draw_acts(key, part):
    shape = (PIPE, CLIPS, FRAMES, POS, C)
    first_key = jax.random.fold_in(key, 0)
    result = jax.random.truncated_normal(first_key, -6.0, 6.0, shape, jnp.float32)
    return result.astype(jnp.bfloat16)


def block_levels(rng, extent, cuts, smallest, high):
    def one(dim, blocks):
        steps = jax.random.uniform(jax.random.fold_in(jax.random.fold_in(rng, 6), dim), (blocks,), jnp.float32, smallest / len(cuts), high / len(cuts))
        return jnp.repeat(jnp.exp(steps), extent[dim] // blocks).reshape((-1,) + (1,) * (len(extent) - dim - 1))

    gain = one(*cuts[0])
    for cut in cuts[1:]:
        gain = gain * one(*cut)
    return gain


def bell_draw(stream_key, extent, width, reach, cuts=(), held_as=jnp.bfloat16):
    values = width * jax.random.normal(stream_key, extent, jnp.float32)
    if cuts:
        values = values * block_levels(stream_key, extent, cuts, -0.22, 0.18)
    return jnp.clip(values, -reach, reach).astype(held_as)


def setup_inputs(seed: int = 0) -> dict:
    arg_keys = jax.random.split(jax.random.key(seed), 7)
    acts = draw_acts(jax.random.fold_in(arg_keys[6], 71), 0)
    cotangent = bell_draw(arg_keys[1], (PIPE, CLIPS, FRAMES, POS, C), 1.0, 6.0, ((0, 4), (1, 2), (2, 4)))
    w_query = bell_draw(arg_keys[2], (PIPE, C, INNER), C ** -0.5, 0.15625, ((0, 4),))
    w_key = bell_draw(arg_keys[3], (PIPE, C, INNER), C ** -0.5, 0.15625, ((0, 4),))
    w_value = bell_draw(arg_keys[4], (PIPE, C, INNER), C ** -0.5, 0.15625, ((0, 4),))
    w_out = bell_draw(arg_keys[5], (PIPE, C, INNER), INNER ** -0.5, 0.21875, ((0, 4),))
    return {"acts": acts, "cotangent": cotangent, "w_query": w_query, "w_key": w_key, "w_value": w_value, "w_out": w_out}


score_scale = 0.125


def flatten_rows(array):
    return array.reshape(-1, array.shape[-1])


def attend_back(inputs, projected, w_query, w_key, w_value):
    frames = inputs.shape[0]
    places = inputs.shape[1]

    def project_heads(weight):
        result = jnp.dot(inputs, weight, preferred_element_type=jnp.float32).astype(jnp.bfloat16)
        return result.reshape(frames, places, HEADS, HEAD_DIM)

    queries = project_heads(w_query)
    key_rows = project_heads(w_key)
    values = project_heads(w_value)
    query_full = queries.astype(jnp.float32)
    key_full = key_rows.astype(jnp.float32)
    value_full = values.astype(jnp.float32)
    scores = jnp.einsum("iphd,jphd->phij", query_full, key_full) * score_scale
    probability = jax.nn.softmax(scores, axis=-1)
    prob_short = lax.optimization_barrier(probability.astype(jnp.bfloat16)).astype(jnp.float32)
    proj_full = projected.reshape(frames, places, HEADS, HEAD_DIM).astype(jnp.float32)
    grad_prob = jnp.einsum("iphd,jphd->phij", proj_full, value_full)
    value_grad = jnp.einsum("phij,iphd->jphd", prob_short, proj_full).astype(jnp.bfloat16)
    score_grad = probability * (grad_prob - jnp.sum(grad_prob * probability, axis=-1, keepdims=True))
    score_short = lax.optimization_barrier(score_grad.astype(jnp.bfloat16)).astype(jnp.float32)
    query_grad = (jnp.einsum("phij,jphd->iphd", score_short, key_full) * score_scale).astype(jnp.bfloat16)
    key_grad = (jnp.einsum("phij,iphd->jphd", score_short, query_full) * score_scale).astype(jnp.bfloat16)
    inner = HEADS * HEAD_DIM
    query_grad = query_grad.reshape(frames, places, inner)
    key_grad = key_grad.reshape(frames, places, inner)
    value_grad = value_grad.reshape(frames, places, inner)
    branch = jnp.dot(query_grad, w_query.T, preferred_element_type=jnp.float32)
    branch = branch + jnp.dot(key_grad, w_key.T, preferred_element_type=jnp.float32)
    branch = branch + jnp.dot(value_grad, w_value.T, preferred_element_type=jnp.float32)
    branch = branch.astype(jnp.bfloat16)
    weight_grad = jnp.dot(flatten_rows(inputs).T, flatten_rows(value_grad), preferred_element_type=jnp.float32)
    return branch, weight_grad


def clip_terms(inputs, upstream, w_query, w_key, w_value, w_out):
    projected = jnp.dot(upstream, w_out, preferred_element_type=jnp.float32).astype(jnp.bfloat16)
    branch, value_part = attend_back(inputs, projected, w_query, w_key, w_value)
    input_grad = (upstream.astype(jnp.float32) + branch.astype(jnp.float32)).astype(jnp.bfloat16)
    return input_grad, value_part


def reference(acts, cotangent, w_query, w_key, w_value, w_out):
    def section(packed):
        inputs, upstream, query_weight, key_weight, value_weight, out_weight = packed

        def one_clip(pair):
            return clip_terms(pair[0], pair[1], query_weight, key_weight, value_weight, out_weight)

        input_grad, value_parts = lax.map(one_clip, (inputs, upstream))
        return input_grad, jnp.sum(value_parts, axis=0)

    input_grad, grad_value = lax.map(section, (acts, cotangent, w_query, w_key, w_value, w_out))
    sent_grad = jnp.concatenate([input_grad[1:], jnp.zeros_like(input_grad[:1])], axis=0)
    return sent_grad, grad_value
```

```python
import functools

import jax
import jax.numpy as jnp
from jax import lax
from jax.experimental import pallas as pl
from jax.experimental.pallas import tpu as pltpu
from jax.sharding import PartitionSpec as P

HEADS = 12
HEAD_DIM = 64


score_scale = 0.125


def shifted(shard, axis, by):
    count = lax.axis_size(axis)
    pairs = [(i, i + by) for i in range(count) if 0 <= i + by < count]
    return lax.ppermute(shard, axis, pairs)


def rotated(shard, axis, by):
    count = lax.axis_size(axis)
    return lax.ppermute(shard, axis, [(i, (i + by) % count) for i in range(count)])


def attend_back(inputs, projected, w_query, w_key, w_value):
    frames = inputs.shape[0]
    places = inputs.shape[1]

    def project_heads(weight):
        result = jnp.dot(inputs, weight, preferred_element_type=jnp.float32).astype(jnp.bfloat16)
        return result.reshape(frames, places, HEADS, HEAD_DIM)

    queries = project_heads(w_query)
    key_rows = project_heads(w_key)
    values = project_heads(w_value)
    scores = (
        jnp.einsum("iphd,jphd->phij", queries, key_rows, preferred_element_type=jnp.float32)
        * score_scale
    )
    probability = jax.nn.softmax(scores, axis=-1)
    prob_short = probability.astype(jnp.bfloat16)
    proj_heads = projected.reshape(frames, places, HEADS, HEAD_DIM)
    grad_prob = jnp.einsum(
        "iphd,jphd->phij", proj_heads, values, preferred_element_type=jnp.float32
    )
    value_grad = jnp.einsum(
        "phij,iphd->jphd", prob_short, proj_heads, preferred_element_type=jnp.float32
    ).astype(jnp.bfloat16)
    score_grad = probability * (
        grad_prob - jnp.sum(grad_prob * probability, axis=-1, keepdims=True)
    )
    score_short = score_grad.astype(jnp.bfloat16)
    query_grad = (
        jnp.einsum("phij,jphd->iphd", score_short, key_rows, preferred_element_type=jnp.float32)
        * score_scale
    ).astype(jnp.bfloat16)
    key_grad = (
        jnp.einsum("phij,iphd->jphd", score_short, queries, preferred_element_type=jnp.float32)
        * score_scale
    ).astype(jnp.bfloat16)
    inner = HEADS * HEAD_DIM
    query_grad = query_grad.reshape(frames, places, inner)
    key_grad = key_grad.reshape(frames, places, inner)
    value_grad = value_grad.reshape(frames, places, inner)
    branch = jnp.einsum("fpj,cj->fpc", query_grad, w_query, preferred_element_type=jnp.float32)
    branch = branch + jnp.einsum("fpj,cj->fpc", key_grad, w_key, preferred_element_type=jnp.float32)
    branch = branch + jnp.einsum(
        "fpj,cj->fpc", value_grad, w_value, preferred_element_type=jnp.float32
    )
    branch = branch.astype(jnp.bfloat16)
    weight_grad = jnp.einsum("fpc,fpj->cj", inputs, value_grad, preferred_element_type=jnp.float32)
    return (branch, weight_grad)


def general_body(acts, cotangent, w_query, w_key, w_value, w_out):
    inputs = acts[0, 0]
    upstream = cotangent[0, 0]
    row_inputs, row_upstream = (
        lax.all_to_all(inputs, "frame", split_axis=1, concat_axis=0, tiled=True),
        lax.all_to_all(upstream, "frame", split_axis=1, concat_axis=0, tiled=True),
    )
    projected = jnp.dot(row_upstream, w_out[0], preferred_element_type=jnp.float32).astype(
        jnp.bfloat16
    )
    branch, value_grad = attend_back(row_inputs, projected, w_query[0], w_key[0], w_value[0])
    row_result = (row_upstream.astype(jnp.float32) + branch.astype(jnp.float32)).astype(
        jnp.bfloat16
    )
    frame_result = lax.all_to_all(row_result, "frame", split_axis=0, concat_axis=1, tiled=True)
    sent_grad = shifted(frame_result[None, None], "pipe", -1)
    value_middle = lax.psum_scatter(
        value_grad.astype(jnp.bfloat16), "frame", scatter_dimension=1, tiled=True
    )
    value_part = lax.psum_scatter(value_middle, "dp", scatter_dimension=1, tiled=True).astype(
        jnp.float32
    )
    return (sent_grad, value_part[None])


def flat_rows(ref):
    block = ref[...]
    frames, places, channels = block.shape
    flat = block.astype(jnp.float32).reshape(frames * places, channels)
    return flat.astype(jnp.bfloat16)


def dot_nn(a, b):
    return jnp.dot(a, b, preferred_element_type=jnp.float32)


def dot_nt(a, b):
    return lax.dot_general(a, b, (((1,), (1,)), ((), ())), preferred_element_type=jnp.float32)


def dot_tn(a, b):
    return lax.dot_general(a, b, (((0,), (0,)), ((), ())), preferred_element_type=jnp.float32)


def project_kernel(upstream_ref, weight_ref, out_ref):
    out_ref[...] = dot_nn(flat_rows(upstream_ref), weight_ref[...]).astype(jnp.bfloat16)


def pair_rows(pair):
    lane = lax.broadcasted_iota(jnp.int32, pair.shape, 1)
    wide = pair.astype(jnp.float32)
    first = jnp.where(lane < HEAD_DIM, wide, 0.0).astype(jnp.bfloat16)
    second = jnp.where(lane < HEAD_DIM, 0.0, wide).astype(jnp.bfloat16)
    return jnp.concatenate([first, second], axis=0)


def forward_kernel(blocks, places, *refs):
    act_refs = refs[:blocks]
    weight_refs = refs[blocks : blocks + 3]
    row_ref, q_ref, k_ref, v_ref, prob_ref, held, sems = refs[blocks + 3 :]
    copies = [
        pltpu.make_async_copy(weight_refs[i], held.at[i], sems.at[i]) for i in range(3)
    ]
    for copy in copies:
        copy.start()
    rows = jnp.concatenate([flat_rows(ref) for ref in act_refs], axis=0)
    row_ref[...] = rows
    for i, out_ref in enumerate((q_ref, k_ref, v_ref)):
        copies[i].wait()
        out_ref[...] = dot_nn(rows, held[i]).astype(jnp.bfloat16)
    count = rows.shape[0]
    row = lax.broadcasted_iota(jnp.int32, (count, 2 * count), 0)
    col = lax.broadcasted_iota(jnp.int32, (count, 2 * count), 1)
    same = lax.rem(row, places) == lax.rem(col, places)
    width = 2 * HEAD_DIM
    for pair in range(HEADS // 2):
        at = pl.ds(pair * width, width)
        scores = dot_nt(k_ref[:, at], pair_rows(q_ref[:, at])) * score_scale
        scores = jnp.where(same, scores, -jnp.inf)
        top = jnp.max(scores, axis=0, keepdims=True)
        raised = jnp.exp(scores - top)
        prob_ref[pair] = raised / jnp.sum(raised, axis=0, keepdims=True)


def backward_kernel(blocks, own, shares, *refs):
    proj_refs = refs[:blocks]
    q_ref, k_ref, v_ref, prob_ref, upstream_ref, *weight_refs = refs[blocks : blocks + 8]
    out_ref, mine_ref, send_ref, proj, grads, vgrad, held, sems = refs[blocks + 8 :]
    copies = [
        pltpu.make_async_copy(weight_refs[i], held.at[i], sems.at[i]) for i in range(3)
    ]
    for copy in copies:
        copy.start()
    for i, ref in enumerate(proj_refs):
        proj[i * own : (i + 1) * own, :] = ref[...]
    count = proj.shape[0]
    width = 2 * HEAD_DIM
    lane = lax.broadcasted_iota(jnp.int32, (own, width), 1)
    for pair in range(HEADS // 2):
        at = pl.ds(pair * width, width)
        prob = prob_ref[pair]
        proj_pair = pair_rows(proj[:, at])
        grad_prob = dot_nt(v_ref[:, at], proj_pair)
        mean = jnp.sum(grad_prob * prob, axis=0, keepdims=True)
        score_grad = (prob * (grad_prob - mean)).astype(jnp.bfloat16)
        vgrad[:, at] = dot_nn(prob.astype(jnp.bfloat16), proj_pair).astype(jnp.bfloat16)
        key_grad = dot_nn(score_grad[:own], pair_rows(q_ref[:, at])) * score_scale
        grads[1, :, at] = key_grad.astype(jnp.bfloat16)
        keys = k_ref[:, at]
        first = dot_tn(score_grad[:, :own], keys)
        second = dot_tn(score_grad[:, count : count + own], keys)
        query_grad = jnp.where(lane < HEAD_DIM, first, second) * score_scale
        grads[0, :, at] = query_grad.astype(jnp.bfloat16)
    frame, member = lax.axis_index("frame"), lax.axis_index("dp")
    inner = HEADS * HEAD_DIM
    share = inner // shares
    mine = (frame * lax.axis_size("dp") + member) * share
    other = (frame * lax.axis_size("dp") + 1 - member) * share
    pick_row = lax.broadcasted_iota(jnp.int32, (inner, 128), 0)
    pick_col = lax.broadcasted_iota(jnp.int32, (inner, 128), 1)

    def picked(start):
        chosen = (pick_row - pick_col == start) & (pick_col < share)
        pick = jnp.where(chosen, 1.0, 0.0).astype(jnp.bfloat16)
        return dot_nn(vgrad[...], pick).astype(jnp.bfloat16)

    mine_ref[...] = picked(mine)
    send_ref[...] = picked(other)
    copies[0].wait()
    branch = dot_nt(grads[0], held[0])
    copies[1].wait()
    branch = branch + dot_nt(grads[1], held[1])
    copies[2].wait()
    branch = branch + dot_nt(vgrad[:own, :], held[2])
    branch = branch.astype(jnp.bfloat16).astype(jnp.float32)
    result = flat_rows(upstream_ref).astype(jnp.float32) + branch
    out_ref[...] = result.reshape(out_ref.shape).astype(jnp.bfloat16)


def gradient_kernel(rows_ref, mine_ref, *refs):
    *act_refs, other_ref, out_ref = refs
    others = jnp.concatenate([flat_rows(ref) for ref in act_refs], axis=0)
    total = dot_tn(rows_ref[...], mine_ref[...]) + dot_tn(others, other_ref[...])
    out_ref[...] = total[:, : out_ref.shape[1]]


VMEM = pl.BlockSpec(memory_space=pltpu.VMEM)
ANY = pl.BlockSpec(memory_space=pl.ANY)


def few_rows_body(acts, cotangent, w_query, w_key, w_value, w_out):
    inputs = acts[0, 0]
    upstream = cotangent[0, 0]
    frames, places, channels = inputs.shape
    inner = w_query.shape[-1]
    count = lax.axis_size("frame")
    shares = count * lax.axis_size("dp")
    own = frames * places
    rows = count * own
    bf16 = jnp.bfloat16
    weights = (w_query[0], w_key[0], w_value[0])
    shape = jax.ShapeDtypeStruct
    turns = range(count - 1, 0, -1)

    blocks = [inputs] + [rotated(inputs, "frame", turn) for turn in turns]
    others = [rotated(block, "dp", 1) for block in blocks]
    projected = pl.pallas_call(
        project_kernel,
        out_shape=shape((own, inner), bf16),
        in_specs=[VMEM, VMEM],
        out_specs=VMEM,
        name="project",
    )(upstream, w_out[0])
    all_projected = [projected] + [rotated(projected, "frame", turn) for turn in turns]

    pairs = HEADS // 2
    flat, queries, key_rows, values, probability = pl.pallas_call(
        functools.partial(forward_kernel, count, places),
        out_shape=(
            shape((rows, channels), bf16),
            shape((rows, inner), bf16),
            shape((rows, inner), bf16),
            shape((rows, inner), bf16),
            shape((pairs, rows, 2 * rows), jnp.float32),
        ),
        in_specs=[VMEM] * count + [ANY] * 3,
        out_specs=(VMEM,) * 5,
        scratch_shapes=[
            pltpu.VMEM((3, channels, inner), bf16),
            pltpu.SemaphoreType.DMA((3,)),
        ],
        name="forward",
    )(*blocks, *weights)
    result, mine, send = pl.pallas_call(
        functools.partial(backward_kernel, count, own, shares),
        out_shape=(
            shape((frames, places, channels), bf16),
            shape((rows, 128), bf16),
            shape((rows, 128), bf16),
        ),
        in_specs=[VMEM] * (count + 5) + [ANY] * 3,
        out_specs=(VMEM,) * 3,
        scratch_shapes=[
            pltpu.VMEM((rows, inner), bf16),
            pltpu.VMEM((2, own, inner), bf16),
            pltpu.VMEM((rows, inner), bf16),
            pltpu.VMEM((3, channels, inner), bf16),
            pltpu.SemaphoreType.DMA((3,)),
        ],
        name="backward",
    )(*all_projected, queries, key_rows, values, probability, upstream, *weights)
    sent_grad = shifted(result, "pipe", -1)
    received = rotated(send, "dp", 1)
    value_part = pl.pallas_call(
        gradient_kernel,
        out_shape=shape((channels, inner // shares), jnp.float32),
        in_specs=[VMEM] * (count + 3),
        out_specs=VMEM,
        name="gradient",
    )(flat, mine, *others, received)
    return (sent_grad[None, None], value_part[None])


def body(acts, cotangent, *weights):
    count, members = lax.axis_size("frame"), lax.axis_size("dp")
    rows = count * acts.shape[2] * acts.shape[3]
    share = weights[0].shape[-1] // (count * members)
    few = members == 2 and rows <= 128 and share <= 128 and HEADS % 2 == 0
    return (few_rows_body if few else general_body)(acts, cotangent, *weights)


def solution(mesh):
    return jax.shard_map(
        body,
        mesh=mesh,
        in_specs=(
            P("pipe", "dp", "frame", None, None),
            P("pipe", "dp", "frame", None, None),
            P("pipe", None, None),
            P("pipe", None, None),
            P("pipe", None, None),
            P("pipe", None, None),
        ),
        out_specs=(P("pipe", "dp", "frame", None, None), P("pipe", None, ("frame", "dp"))),
        check_vma=False,
    )
```

```python
import functools

import jax
import jax.numpy as jnp
from jax import lax
from jax.experimental import pallas as pl
from jax.experimental.pallas import tpu as pltpu
from jax.sharding import PartitionSpec as P


HEADS = 12
HEAD_DIM = 64


score_scale = 0.125


def shifted(shard, axis, by):
    count = lax.axis_size(axis)
    pairs = [(i, i + by) for i in range(count) if 0 <= i + by < count]
    return lax.ppermute(shard, axis, pairs)


def rotated(shard, axis, by):
    count = lax.axis_size(axis)
    return lax.ppermute(shard, axis, [(i, (i + by) % count) for i in range(count)])


def attend_back(inputs, projected, w_query, w_key, w_value):
    frames = inputs.shape[0]
    places = inputs.shape[1]

    def project_heads(weight):
        result = jnp.dot(inputs, weight, preferred_element_type=jnp.float32).astype(jnp.bfloat16)
        return result.reshape(frames, places, HEADS, HEAD_DIM)

    queries = project_heads(w_query)
    key_rows = project_heads(w_key)
    values = project_heads(w_value)
    scores = (
        jnp.einsum("iphd,jphd->phij", queries, key_rows, preferred_element_type=jnp.float32)
        * score_scale
    )
    probability = jax.nn.softmax(scores, axis=-1)
    prob_short = probability.astype(jnp.bfloat16)
    proj_heads = projected.reshape(frames, places, HEADS, HEAD_DIM)
    grad_prob = jnp.einsum(
        "iphd,jphd->phij", proj_heads, values, preferred_element_type=jnp.float32
    )
    value_grad = jnp.einsum(
        "phij,iphd->jphd", prob_short, proj_heads, preferred_element_type=jnp.float32
    ).astype(jnp.bfloat16)
    score_grad = probability * (
        grad_prob - jnp.sum(grad_prob * probability, axis=-1, keepdims=True)
    )
    score_short = score_grad.astype(jnp.bfloat16)
    query_grad = (
        jnp.einsum("phij,jphd->iphd", score_short, key_rows, preferred_element_type=jnp.float32)
        * score_scale
    ).astype(jnp.bfloat16)
    key_grad = (
        jnp.einsum("phij,iphd->jphd", score_short, queries, preferred_element_type=jnp.float32)
        * score_scale
    ).astype(jnp.bfloat16)
    inner = HEADS * HEAD_DIM
    query_grad = query_grad.reshape(frames, places, inner)
    key_grad = key_grad.reshape(frames, places, inner)
    value_grad = value_grad.reshape(frames, places, inner)
    branch = jnp.einsum("fpj,cj->fpc", query_grad, w_query, preferred_element_type=jnp.float32)
    branch = branch + jnp.einsum("fpj,cj->fpc", key_grad, w_key, preferred_element_type=jnp.float32)
    branch = branch + jnp.einsum(
        "fpj,cj->fpc", value_grad, w_value, preferred_element_type=jnp.float32
    )
    branch = branch.astype(jnp.bfloat16)
    weight_grad = jnp.einsum("fpc,fpj->cj", inputs, value_grad, preferred_element_type=jnp.float32)
    return (branch, weight_grad)


def general_body(acts, cotangent, w_query, w_key, w_value, w_out):
    inputs = acts[0, 0]
    upstream = cotangent[0, 0]
    row_inputs, row_upstream = (
        lax.all_to_all(inputs, "frame", split_axis=1, concat_axis=0, tiled=True),
        lax.all_to_all(upstream, "frame", split_axis=1, concat_axis=0, tiled=True),
    )
    projected = jnp.dot(row_upstream, w_out[0], preferred_element_type=jnp.float32).astype(
        jnp.bfloat16
    )
    branch, value_grad = attend_back(row_inputs, projected, w_query[0], w_key[0], w_value[0])
    row_result = (row_upstream.astype(jnp.float32) + branch.astype(jnp.float32)).astype(
        jnp.bfloat16
    )
    frame_result = lax.all_to_all(row_result, "frame", split_axis=0, concat_axis=1, tiled=True)
    sent_grad = shifted(frame_result[None, None], "pipe", -1)
    value_middle = lax.psum_scatter(
        value_grad.astype(jnp.bfloat16), "frame", scatter_dimension=1, tiled=True
    )
    value_part = lax.psum_scatter(value_middle, "dp", scatter_dimension=1, tiled=True).astype(
        jnp.float32
    )
    return (sent_grad, value_part[None])


def flat_rows(ref):
    block = ref[...]
    frames, places, channels = block.shape
    flat = block.astype(jnp.float32).reshape(frames * places, channels)
    return flat.astype(jnp.bfloat16)


def dot_nn(a, b):
    return jnp.dot(a, b, preferred_element_type=jnp.float32)


def dot_nt(a, b):
    return lax.dot_general(a, b, (((1,), (1,)), ((), ())), preferred_element_type=jnp.float32)


def dot_tn(a, b):
    return lax.dot_general(a, b, (((0,), (0,)), ((), ())), preferred_element_type=jnp.float32)


def project_kernel(upstream_ref, weight_ref, out_ref):
    out_ref[...] = dot_nn(flat_rows(upstream_ref), weight_ref[...]).astype(jnp.bfloat16)


def pair_rows(pair):
    lane = lax.broadcasted_iota(jnp.int32, pair.shape, 1)
    wide = pair.astype(jnp.float32)
    first = jnp.where(lane < HEAD_DIM, wide, 0.0).astype(jnp.bfloat16)
    second = jnp.where(lane < HEAD_DIM, 0.0, wide).astype(jnp.bfloat16)
    return jnp.concatenate([first, second], axis=0)


def flatten_kernel(*refs):
    *act_refs, out_ref = refs
    own = out_ref.shape[0] // len(act_refs)
    for i, ref in enumerate(act_refs):
        out_ref[i * own : (i + 1) * own, :] = flat_rows(ref)


def forward_kernel(places, *refs):
    row_ref, *weight_refs = refs[:4]
    q_ref, k_ref, v_ref, prob_ref, held, sems = refs[4:]
    copies = [
        pltpu.make_async_copy(weight_refs[i], held.at[i], sems.at[i]) for i in range(3)
    ]
    for copy in copies:
        copy.start()
    rows = row_ref[...]
    for i, out_ref in enumerate((q_ref, k_ref, v_ref)):
        copies[i].wait()
        out_ref[...] = dot_nn(rows, held[i]).astype(jnp.bfloat16)
    count = rows.shape[0]
    row = lax.broadcasted_iota(jnp.int32, (count, 2 * count), 0)
    col = lax.broadcasted_iota(jnp.int32, (count, 2 * count), 1)
    same = lax.rem(row, places) == lax.rem(col, places)
    width = 2 * HEAD_DIM
    for pair in range(HEADS // 2):
        at = pl.ds(pair * width, width)
        scores = dot_nt(k_ref[:, at], pair_rows(q_ref[:, at])) * score_scale
        scores = jnp.where(same, scores, -jnp.inf)
        top = jnp.max(scores, axis=0, keepdims=True)
        raised = jnp.exp(scores - top)
        prob_ref[pair] = raised / jnp.sum(raised, axis=0, keepdims=True)


def value_kernel(blocks, shares, *refs):
    prob_ref, *proj_refs = refs[: blocks + 1]
    proj_ref, own_ref, mine_ref, send_ref, vgrad = refs[blocks + 1 :]
    own = own_ref.shape[0]
    for i, ref in enumerate(proj_refs):
        proj_ref[i * own : (i + 1) * own, :] = ref[...]
    width = 2 * HEAD_DIM
    for pair in range(HEADS // 2):
        at = pl.ds(pair * width, width)
        short = prob_ref[pair].astype(jnp.bfloat16)
        vgrad[:, at] = dot_nn(short, pair_rows(proj_ref[:, at])).astype(jnp.bfloat16)
    own_ref[...] = vgrad[:own, :]
    frame, member = lax.axis_index("frame"), lax.axis_index("dp")
    inner = HEADS * HEAD_DIM
    share = inner // shares
    pick_row = lax.broadcasted_iota(jnp.int32, (inner, 128), 0)
    pick_col = lax.broadcasted_iota(jnp.int32, (inner, 128), 1)

    def picked(start):
        chosen = (pick_row - pick_col == start) & (pick_col < share)
        pick = jnp.where(chosen, 1.0, 0.0).astype(jnp.bfloat16)
        return dot_nn(vgrad[...], pick).astype(jnp.bfloat16)

    mine_ref[...] = picked((frame * lax.axis_size("dp") + member) * share)
    send_ref[...] = picked((frame * lax.axis_size("dp") + 1 - member) * share)


def backward_kernel(*refs):
    prob_ref, q_ref, k_ref, v_ref, proj_ref, vgrad_ref, upstream_ref, *weight_refs = refs[:10]
    out_ref, grads, held, sems = refs[10:]
    copies = [
        pltpu.make_async_copy(weight_refs[i], held.at[i], sems.at[i]) for i in (2, 0, 1)
    ]
    for copy in copies:
        copy.start()
    count = proj_ref.shape[0]
    own = vgrad_ref.shape[0]
    width = 2 * HEAD_DIM
    lane = lax.broadcasted_iota(jnp.int32, (own, width), 1)
    for pair in range(HEADS // 2):
        at = pl.ds(pair * width, width)
        prob = prob_ref[pair]
        grad_prob = dot_nt(v_ref[:, at], pair_rows(proj_ref[:, at]))
        mean = jnp.sum(grad_prob * prob, axis=0, keepdims=True)
        score_grad = (prob * (grad_prob - mean)).astype(jnp.bfloat16)
        key_grad = dot_nn(score_grad[:own], pair_rows(q_ref[:, at])) * score_scale
        grads[1, :, at] = key_grad.astype(jnp.bfloat16)
        keys = k_ref[:, at]
        first = dot_tn(score_grad[:, :own], keys)
        second = dot_tn(score_grad[:, count : count + own], keys)
        query_grad = jnp.where(lane < HEAD_DIM, first, second) * score_scale
        grads[0, :, at] = query_grad.astype(jnp.bfloat16)
    copies[0].wait()
    branch = dot_nt(vgrad_ref[...], held[2])
    copies[1].wait()
    branch = branch + dot_nt(grads[0], held[0])
    copies[2].wait()
    branch = branch + dot_nt(grads[1], held[1])
    branch = branch.astype(jnp.bfloat16).astype(jnp.float32)
    result = flat_rows(upstream_ref).astype(jnp.float32) + branch
    out_ref[...] = result.reshape(out_ref.shape).astype(jnp.bfloat16)


def gradient_kernel(row_ref, mine_ref, other_row_ref, other_ref, out_ref):
    total = dot_tn(mine_ref[...], row_ref[...]) + dot_tn(other_ref[...], other_row_ref[...])
    out_ref[...] = total[: out_ref.shape[0]]


VMEM = pl.BlockSpec(memory_space=pltpu.VMEM)
ANY = pl.BlockSpec(memory_space=pl.ANY)


def call(kernel, out_shape, in_specs, scratch=(), grant=24):
    return pl.pallas_call(
        kernel,
        out_shape=out_shape,
        in_specs=in_specs,
        out_specs=jax.tree.map(lambda _: VMEM, out_shape),
        scratch_shapes=scratch,
        compiler_params=pltpu.CompilerParams(vmem_limit_bytes=grant * 2**20),
    )


def few_rows_body(acts, cotangent, w_query, w_key, w_value, w_out):
    inputs = acts[0, 0]
    upstream = cotangent[0, 0]
    frames, places, channels = inputs.shape
    inner = w_query.shape[-1]
    count = lax.axis_size("frame")
    shares = count * lax.axis_size("dp")
    own = frames * places
    rows = count * own
    bf16 = jnp.bfloat16
    weights = (w_query[0], w_key[0], w_value[0])
    shape = jax.ShapeDtypeStruct
    turns = range(count - 1, 0, -1)
    held = [pltpu.VMEM((3, channels, inner), bf16), pltpu.SemaphoreType.DMA((3,))]

    def gathered(block):
        received = [block]
        for turn in turns:
            received.append(rotated(block, "frame", turn))
        return received

    blocks = gathered(inputs)
    projected = call(project_kernel, shape((own, inner), bf16), [VMEM, VMEM])(upstream, w_out[0])
    all_projected = gathered(projected)
    flat = call(flatten_kernel, shape((rows, channels), bf16), [VMEM] * count)(*blocks)
    other_flat = rotated(flat, "dp", 1)
    wide = shape((rows, inner), bf16)
    queries, key_rows, values, probability = call(
        functools.partial(forward_kernel, places),
        (wide, wide, wide, shape((HEADS // 2, rows, 2 * rows), jnp.float32)),
        [VMEM] + [ANY] * 3,
        held,
    )(flat, *weights)
    narrow = shape((rows, 128), bf16)
    joined, vgrad, mine, send = call(
        functools.partial(value_kernel, count, shares),
        (wide, shape((own, inner), bf16), narrow, narrow),
        [VMEM] * (count + 1),
        [pltpu.VMEM((rows, inner), bf16)],
    )(probability, *all_projected)
    received = rotated(send, "dp", 1)
    result = call(
        backward_kernel,
        shape((frames, places, channels), bf16),
        [VMEM] * 7 + [ANY] * 3,
        [pltpu.VMEM((2, own, inner), bf16)] + held,
    )(probability, queries, key_rows, values, joined, vgrad, upstream, *weights)
    sent_grad = shifted(result, "pipe", -1)
    value_part = call(
        gradient_kernel, shape((inner // shares, channels), jnp.float32), [VMEM] * 4
    )(flat, mine, other_flat, received)
    return (sent_grad[None, None], value_part.T[None])


def few_rows(mesh, acts, inner):
    count, members = mesh.shape["frame"], mesh.shape["dp"]
    rows = acts.shape[2] * acts.shape[3]
    share = inner // (count * members)
    return members == 2 and rows <= 128 and share <= 128 and HEADS % 2 == 0


def solution(mesh):
    specs = (P("pipe", "dp", "frame", None, None),) * 2 + (P("pipe", None, None),) * 4

    def sharded(body):
        return jax.shard_map(
            body,
            mesh=mesh,
            in_specs=specs,
            out_specs=(specs[0], P("pipe", None, ("frame", "dp"))),
            check_vma=False,
        )

    def program(acts, cotangent, *weights):
        if few_rows(mesh, acts, weights[0].shape[-1]):
            return sharded(few_rows_body)(acts, cotangent, *weights)
        return sharded(general_body)(acts, cotangent, *weights)

    return program
```

```python
import functools

import jax
import jax.numpy as jnp
from jax import lax
from jax.experimental import pallas as pl
from jax.experimental.pallas import tpu as pltpu
from jax.sharding import PartitionSpec as P


HEADS = 12
HEAD_DIM = 64


score_scale = 0.125


def shifted(shard, axis, by):
    count = lax.axis_size(axis)
    pairs = [(i, i + by) for i in range(count) if 0 <= i + by < count]
    return lax.ppermute(shard, axis, pairs)


def rotated(shard, axis, by):
    count = lax.axis_size(axis)
    return lax.ppermute(shard, axis, [(i, (i + by) % count) for i in range(count)])


def attend_back(inputs, projected, w_query, w_key, w_value):
    frames = inputs.shape[0]
    places = inputs.shape[1]

    def project_heads(weight):
        result = jnp.dot(inputs, weight, preferred_element_type=jnp.float32).astype(jnp.bfloat16)
        return result.reshape(frames, places, HEADS, HEAD_DIM)

    queries = project_heads(w_query)
    key_rows = project_heads(w_key)
    values = project_heads(w_value)
    scores = (
        jnp.einsum("iphd,jphd->phij", queries, key_rows, preferred_element_type=jnp.float32)
        * score_scale
    )
    probability = jax.nn.softmax(scores, axis=-1)
    prob_short = probability.astype(jnp.bfloat16)
    proj_heads = projected.reshape(frames, places, HEADS, HEAD_DIM)
    grad_prob = jnp.einsum(
        "iphd,jphd->phij", proj_heads, values, preferred_element_type=jnp.float32
    )
    value_grad = jnp.einsum(
        "phij,iphd->jphd", prob_short, proj_heads, preferred_element_type=jnp.float32
    ).astype(jnp.bfloat16)
    score_grad = probability * (
        grad_prob - jnp.sum(grad_prob * probability, axis=-1, keepdims=True)
    )
    score_short = score_grad.astype(jnp.bfloat16)
    query_grad = (
        jnp.einsum("phij,jphd->iphd", score_short, key_rows, preferred_element_type=jnp.float32)
        * score_scale
    ).astype(jnp.bfloat16)
    key_grad = (
        jnp.einsum("phij,iphd->jphd", score_short, queries, preferred_element_type=jnp.float32)
        * score_scale
    ).astype(jnp.bfloat16)
    inner = HEADS * HEAD_DIM
    query_grad = query_grad.reshape(frames, places, inner)
    key_grad = key_grad.reshape(frames, places, inner)
    value_grad = value_grad.reshape(frames, places, inner)
    branch = jnp.einsum("fpj,cj->fpc", query_grad, w_query, preferred_element_type=jnp.float32)
    branch = branch + jnp.einsum("fpj,cj->fpc", key_grad, w_key, preferred_element_type=jnp.float32)
    branch = branch + jnp.einsum(
        "fpj,cj->fpc", value_grad, w_value, preferred_element_type=jnp.float32
    )
    branch = branch.astype(jnp.bfloat16)
    weight_grad = jnp.einsum("fpc,fpj->cj", inputs, value_grad, preferred_element_type=jnp.float32)
    return (branch, weight_grad)


def general_body(acts, cotangent, w_query, w_key, w_value, w_out):
    inputs = acts[0, 0]
    upstream = cotangent[0, 0]
    row_inputs, row_upstream = (
        lax.all_to_all(inputs, "frame", split_axis=1, concat_axis=0, tiled=True),
        lax.all_to_all(upstream, "frame", split_axis=1, concat_axis=0, tiled=True),
    )
    projected = jnp.dot(row_upstream, w_out[0], preferred_element_type=jnp.float32).astype(
        jnp.bfloat16
    )
    branch, value_grad = attend_back(row_inputs, projected, w_query[0], w_key[0], w_value[0])
    row_result = (row_upstream.astype(jnp.float32) + branch.astype(jnp.float32)).astype(
        jnp.bfloat16
    )
    frame_result = lax.all_to_all(row_result, "frame", split_axis=0, concat_axis=1, tiled=True)
    sent_grad = shifted(frame_result[None, None], "pipe", -1)
    value_middle = lax.psum_scatter(
        value_grad.astype(jnp.bfloat16), "frame", scatter_dimension=1, tiled=True
    )
    value_part = lax.psum_scatter(value_middle, "dp", scatter_dimension=1, tiled=True).astype(
        jnp.float32
    )
    return (sent_grad, value_part[None])


def flat_rows(ref):
    block = ref[...]
    frames, places, channels = block.shape
    flat = block.astype(jnp.float32).reshape(frames * places, channels)
    return flat.astype(jnp.bfloat16)


def dot_nn(a, b):
    return jnp.dot(a, b, preferred_element_type=jnp.float32)


def dot_nt(a, b):
    return lax.dot_general(a, b, (((1,), (1,)), ((), ())), preferred_element_type=jnp.float32)


def dot_tn(a, b):
    return lax.dot_general(a, b, (((0,), (0,)), ((), ())), preferred_element_type=jnp.float32)


def project_kernel(upstream_ref, weight_ref, out_ref):
    out_ref[...] = dot_nn(flat_rows(upstream_ref), weight_ref[...]).astype(jnp.bfloat16)


def pair_rows(pair):
    lane = lax.broadcasted_iota(jnp.int32, pair.shape, 1)
    wide = pair.astype(jnp.float32)
    first = jnp.where(lane < HEAD_DIM, wide, 0.0).astype(jnp.bfloat16)
    second = jnp.where(lane < HEAD_DIM, 0.0, wide).astype(jnp.bfloat16)
    return jnp.concatenate([first, second], axis=0)


def flatten_kernel(*refs):
    *act_refs, out_ref = refs
    own = out_ref.shape[0] // len(act_refs)
    for i, ref in enumerate(act_refs):
        out_ref[i * own : (i + 1) * own, :] = flat_rows(ref)


def hold_kernel(*refs):
    *weight_refs, held_ref, sems = refs
    copies = [
        pltpu.make_async_copy(ref, held_ref.at[i], sems.at[i]) for i, ref in enumerate(weight_refs)
    ]
    for copy in copies:
        copy.start()
    for copy in copies:
        copy.wait()


def forward_kernel(places, *refs):
    row_ref, held_ref, q_ref, k_ref, v_ref, prob_ref = refs
    rows = row_ref[...]
    for i, out_ref in enumerate((q_ref, k_ref, v_ref)):
        out_ref[...] = dot_nn(rows, held_ref[i]).astype(jnp.bfloat16)
    count = rows.shape[0]
    row = lax.broadcasted_iota(jnp.int32, (count, 2 * count), 0)
    col = lax.broadcasted_iota(jnp.int32, (count, 2 * count), 1)
    same = lax.rem(row, places) == lax.rem(col, places)
    width = 2 * HEAD_DIM
    for pair in range(HEADS // 2):
        at = pl.ds(pair * width, width)
        scores = dot_nt(k_ref[:, at], pair_rows(q_ref[:, at])) * score_scale
        scores = jnp.where(same, scores, -jnp.inf)
        top = jnp.max(scores, axis=0, keepdims=True)
        raised = jnp.exp(scores - top)
        prob_ref[pair] = raised / jnp.sum(raised, axis=0, keepdims=True)


def value_kernel(blocks, shares, *refs):
    prob_ref, *proj_refs = refs[: blocks + 1]
    proj_ref, own_ref, mine_ref, send_ref, vgrad = refs[blocks + 1 :]
    own = own_ref.shape[0]
    for i, ref in enumerate(proj_refs):
        proj_ref[i * own : (i + 1) * own, :] = ref[...]
    width = 2 * HEAD_DIM
    for pair in range(HEADS // 2):
        at = pl.ds(pair * width, width)
        short = prob_ref[pair].astype(jnp.bfloat16)
        vgrad[:, at] = dot_nn(short, pair_rows(proj_ref[:, at])).astype(jnp.bfloat16)
    own_ref[...] = vgrad[:own, :]
    frame, member = lax.axis_index("frame"), lax.axis_index("dp")
    inner = HEADS * HEAD_DIM
    share = inner // shares
    pick_row = lax.broadcasted_iota(jnp.int32, (inner, 128), 0)
    pick_col = lax.broadcasted_iota(jnp.int32, (inner, 128), 1)

    def picked(start):
        chosen = (pick_row - pick_col == start) & (pick_col < share)
        pick = jnp.where(chosen, 1.0, 0.0).astype(jnp.bfloat16)
        return dot_nn(vgrad[...], pick).astype(jnp.bfloat16)

    mine_ref[...] = picked((frame * lax.axis_size("dp") + member) * share)
    send_ref[...] = picked((frame * lax.axis_size("dp") + 1 - member) * share)


def backward_kernel(*refs):
    prob_ref, q_ref, k_ref, v_ref, proj_ref, vgrad_ref, upstream_ref, held_ref = refs[:8]
    out_ref, grads = refs[8:]
    count = proj_ref.shape[0]
    own = vgrad_ref.shape[0]
    width = 2 * HEAD_DIM
    lane = lax.broadcasted_iota(jnp.int32, (own, width), 1)
    for pair in range(HEADS // 2):
        at = pl.ds(pair * width, width)
        prob = prob_ref[pair]
        grad_prob = dot_nt(v_ref[:, at], pair_rows(proj_ref[:, at]))
        mean = jnp.sum(grad_prob * prob, axis=0, keepdims=True)
        score_grad = (prob * (grad_prob - mean)).astype(jnp.bfloat16)
        key_grad = dot_nn(score_grad[:own], pair_rows(q_ref[:, at])) * score_scale
        grads[1, :, at] = key_grad.astype(jnp.bfloat16)
        keys = k_ref[:, at]
        first = dot_tn(score_grad[:, :own], keys)
        second = dot_tn(score_grad[:, count : count + own], keys)
        query_grad = jnp.where(lane < HEAD_DIM, first, second) * score_scale
        grads[0, :, at] = query_grad.astype(jnp.bfloat16)
    branch = dot_nt(held_ref[2], vgrad_ref[...])
    branch = branch + dot_nt(held_ref[0], grads[0])
    branch = branch + dot_nt(held_ref[1], grads[1])
    branch = branch.T.astype(jnp.bfloat16).astype(jnp.float32)
    result = flat_rows(upstream_ref).astype(jnp.float32) + branch
    out_ref[...] = result.reshape(out_ref.shape).astype(jnp.bfloat16)


def gradient_kernel(row_ref, mine_ref, other_row_ref, other_ref, out_ref):
    total = dot_tn(mine_ref[...], row_ref[...]) + dot_tn(other_ref[...], other_row_ref[...])
    out_ref[...] = total[: out_ref.shape[0]]


VMEM = pl.BlockSpec(memory_space=pltpu.VMEM)
HBM = pl.BlockSpec(memory_space=pltpu.HBM)


def call(kernel, out_shape, in_specs, scratch=(), grant=24):
    return pl.pallas_call(
        kernel,
        out_shape=out_shape,
        in_specs=in_specs,
        out_specs=jax.tree.map(lambda _: VMEM, out_shape),
        scratch_shapes=scratch,
        compiler_params=pltpu.CompilerParams(vmem_limit_bytes=grant * 2**20),
    )


def few_rows_body(acts, cotangent, w_query, w_key, w_value, w_out):
    inputs = acts[0, 0]
    upstream = cotangent[0, 0]
    frames, places, channels = inputs.shape
    inner = w_query.shape[-1]
    count = lax.axis_size("frame")
    shares = count * lax.axis_size("dp")
    own = frames * places
    rows = count * own
    bf16 = jnp.bfloat16
    weights = (w_query[0], w_key[0], w_value[0])
    shape = jax.ShapeDtypeStruct
    turns = range(count - 1, 0, -1)

    def gathered(block):
        received = [block]
        for turn in turns:
            received.append(rotated(block, "frame", turn))
        return received

    blocks = gathered(inputs)
    projected = call(project_kernel, shape((own, inner), bf16), [VMEM, VMEM])(upstream, w_out[0])
    all_projected = gathered(projected)
    held = call(
        hold_kernel,
        shape((3, channels, inner), bf16),
        [HBM] * 3,
        [pltpu.SemaphoreType.DMA((3,))],
        grant=54,
    )(*weights)
    flat = call(flatten_kernel, shape((rows, channels), bf16), [VMEM] * count)(*blocks)
    other_flat = rotated(flat, "dp", 1)
    wide = shape((rows, inner), bf16)
    queries, key_rows, values, probability = call(
        functools.partial(forward_kernel, places),
        (wide, wide, wide, shape((HEADS // 2, rows, 2 * rows), jnp.float32)),
        [VMEM] * 2,
    )(flat, held)
    narrow = shape((rows, 128), bf16)
    joined, vgrad, mine, send = call(
        functools.partial(value_kernel, count, shares),
        (wide, shape((own, inner), bf16), narrow, narrow),
        [VMEM] * (count + 1),
        [pltpu.VMEM((rows, inner), bf16)],
    )(probability, *all_projected)
    received = rotated(send, "dp", 1)
    result = call(
        backward_kernel,
        shape((frames, places, channels), bf16),
        [VMEM] * 8,
        [pltpu.VMEM((2, own, inner), bf16)],
    )(probability, queries, key_rows, values, joined, vgrad, upstream, held)
    sent_grad = shifted(result, "pipe", -1)
    value_part = call(
        gradient_kernel, shape((inner // shares, channels), jnp.float32), [VMEM] * 4
    )(flat, mine, other_flat, received)
    return (sent_grad[None, None], value_part.T[None])


def few_rows(mesh, acts, inner):
    count, members = mesh.shape["frame"], mesh.shape["dp"]
    rows = acts.shape[2] * acts.shape[3]
    share = inner // (count * members)
    return members == 2 and rows <= 128 and share <= 128 and HEADS % 2 == 0


def solution(mesh):
    specs = (P("pipe", "dp", "frame", None, None),) * 2 + (P("pipe", None, None),) * 4

    def sharded(body):
        return jax.shard_map(
            body,
            mesh=mesh,
            in_specs=specs,
            out_specs=(specs[0], P("pipe", None, ("frame", "dp"))),
            check_vma=False,
        )

    def program(acts, cotangent, *weights):
        if few_rows(mesh, acts, weights[0].shape[-1]):
            return sharded(few_rows_body)(acts, cotangent, *weights)
        return sharded(general_body)(acts, cotangent, *weights)

    return program
```

```python
import functools

import jax
import jax.numpy as jnp
from jax import lax
from jax.experimental import pallas as pl
from jax.experimental.pallas import tpu as pltpu
from jax.sharding import PartitionSpec as P


HEADS = 12
HEAD_DIM = 64


score_scale = 0.125


def shifted(shard, axis, by):
    count = lax.axis_size(axis)
    pairs = [(i, i + by) for i in range(count) if 0 <= i + by < count]
    return lax.ppermute(shard, axis, pairs)


def rotated(shard, axis, by):
    count = lax.axis_size(axis)
    return lax.ppermute(shard, axis, [(i, (i + by) % count) for i in range(count)])


def attend_back(inputs, projected, w_query, w_key, w_value):
    frames = inputs.shape[0]
    places = inputs.shape[1]

    def project_heads(weight):
        result = jnp.dot(inputs, weight, preferred_element_type=jnp.float32).astype(jnp.bfloat16)
        return result.reshape(frames, places, HEADS, HEAD_DIM)

    queries = project_heads(w_query)
    key_rows = project_heads(w_key)
    values = project_heads(w_value)
    scores = (
        jnp.einsum("iphd,jphd->phij", queries, key_rows, preferred_element_type=jnp.float32)
        * score_scale
    )
    probability = jax.nn.softmax(scores, axis=-1)
    prob_short = probability.astype(jnp.bfloat16)
    proj_heads = projected.reshape(frames, places, HEADS, HEAD_DIM)
    grad_prob = jnp.einsum(
        "iphd,jphd->phij", proj_heads, values, preferred_element_type=jnp.float32
    )
    value_grad = jnp.einsum(
        "phij,iphd->jphd", prob_short, proj_heads, preferred_element_type=jnp.float32
    ).astype(jnp.bfloat16)
    score_grad = probability * (
        grad_prob - jnp.sum(grad_prob * probability, axis=-1, keepdims=True)
    )
    score_short = score_grad.astype(jnp.bfloat16)
    query_grad = (
        jnp.einsum("phij,jphd->iphd", score_short, key_rows, preferred_element_type=jnp.float32)
        * score_scale
    ).astype(jnp.bfloat16)
    key_grad = (
        jnp.einsum("phij,iphd->jphd", score_short, queries, preferred_element_type=jnp.float32)
        * score_scale
    ).astype(jnp.bfloat16)
    inner = HEADS * HEAD_DIM
    query_grad = query_grad.reshape(frames, places, inner)
    key_grad = key_grad.reshape(frames, places, inner)
    value_grad = value_grad.reshape(frames, places, inner)
    branch = jnp.einsum("fpj,cj->fpc", query_grad, w_query, preferred_element_type=jnp.float32)
    branch = branch + jnp.einsum("fpj,cj->fpc", key_grad, w_key, preferred_element_type=jnp.float32)
    branch = branch + jnp.einsum(
        "fpj,cj->fpc", value_grad, w_value, preferred_element_type=jnp.float32
    )
    branch = branch.astype(jnp.bfloat16)
    weight_grad = jnp.einsum("fpc,fpj->cj", inputs, value_grad, preferred_element_type=jnp.float32)
    return (branch, weight_grad)


def general_body(acts, cotangent, w_query, w_key, w_value, w_out):
    inputs = acts[0, 0]
    upstream = cotangent[0, 0]
    row_inputs, row_upstream = (
        lax.all_to_all(inputs, "frame", split_axis=1, concat_axis=0, tiled=True),
        lax.all_to_all(upstream, "frame", split_axis=1, concat_axis=0, tiled=True),
    )
    projected = jnp.dot(row_upstream, w_out[0], preferred_element_type=jnp.float32).astype(
        jnp.bfloat16
    )
    branch, value_grad = attend_back(row_inputs, projected, w_query[0], w_key[0], w_value[0])
    row_result = (row_upstream.astype(jnp.float32) + branch.astype(jnp.float32)).astype(
        jnp.bfloat16
    )
    frame_result = lax.all_to_all(row_result, "frame", split_axis=0, concat_axis=1, tiled=True)
    sent_grad = shifted(frame_result[None, None], "pipe", -1)
    value_middle = lax.psum_scatter(
        value_grad.astype(jnp.bfloat16), "frame", scatter_dimension=1, tiled=True
    )
    value_part = lax.psum_scatter(value_middle, "dp", scatter_dimension=1, tiled=True).astype(
        jnp.float32
    )
    return (sent_grad, value_part[None])


def flat_rows(ref):
    block = ref[...]
    frames, places, channels = block.shape
    flat = block.astype(jnp.float32).reshape(frames * places, channels)
    return flat.astype(jnp.bfloat16)


def dot_nn(a, b):
    return jnp.dot(a, b, preferred_element_type=jnp.float32)


def dot_nt(a, b):
    return lax.dot_general(a, b, (((1,), (1,)), ((), ())), preferred_element_type=jnp.float32)


def dot_tn(a, b):
    return lax.dot_general(a, b, (((0,), (0,)), ((), ())), preferred_element_type=jnp.float32)


def project_kernel(upstream_ref, *refs):
    *weight_refs, out_ref, row_ref, held_ref, first, upstream, sems = refs
    sources = [upstream_ref, *weight_refs]
    targets = [upstream, first] + [held_ref.at[i] for i in range(3)]
    copies = [
        pltpu.make_async_copy(source, target, sems.at[i])
        for i, (source, target) in enumerate(zip(sources, targets))
    ]
    for copy in copies:
        copy.start()
    copies[0].wait()
    row_ref[...] = flat_rows(upstream)
    copies[1].wait()
    out_ref[...] = dot_nn(row_ref[...], first[...]).astype(jnp.bfloat16)
    for copy in copies[2:]:
        copy.wait()


def pair_rows(pair):
    lane = lax.broadcasted_iota(jnp.int32, pair.shape, 1)
    wide = pair.astype(jnp.float32)
    first = jnp.where(lane < HEAD_DIM, wide, 0.0).astype(jnp.bfloat16)
    second = jnp.where(lane < HEAD_DIM, 0.0, wide).astype(jnp.bfloat16)
    return jnp.concatenate([first, second], axis=0)


def flatten_kernel(*refs):
    *act_refs, out_ref = refs
    own = out_ref.shape[0] // len(act_refs)
    for i, ref in enumerate(act_refs):
        out_ref[i * own : (i + 1) * own, :] = flat_rows(ref)


def forward_kernel(places, *refs):
    row_ref, held_ref, q_ref, k_ref, v_ref, prob_ref = refs
    rows = row_ref[...]
    for i, out_ref in enumerate((q_ref, k_ref, v_ref)):
        out_ref[...] = dot_nn(rows, held_ref[i]).astype(jnp.bfloat16)
    count = rows.shape[0]
    row = lax.broadcasted_iota(jnp.int32, (count, 2 * count), 0)
    col = lax.broadcasted_iota(jnp.int32, (count, 2 * count), 1)
    same = lax.rem(row, places) == lax.rem(col, places)
    width = 2 * HEAD_DIM
    for pair in range(HEADS // 2):
        at = pl.ds(pair * width, width)
        scores = dot_nt(k_ref[:, at], pair_rows(q_ref[:, at])) * score_scale
        scores = jnp.where(same, scores, -jnp.inf)
        top = jnp.max(scores, axis=0, keepdims=True)
        raised = jnp.exp(scores - top)
        prob_ref[pair] = raised / jnp.sum(raised, axis=0, keepdims=True)


def value_kernel(blocks, shares, *refs):
    prob_ref, *proj_refs = refs[: blocks + 1]
    proj_ref, own_ref, mine_ref, send_ref, vgrad = refs[blocks + 1 :]
    own = own_ref.shape[0]
    for i, ref in enumerate(proj_refs):
        proj_ref[i * own : (i + 1) * own, :] = ref[...]
    width = 2 * HEAD_DIM
    for pair in range(HEADS // 2):
        at = pl.ds(pair * width, width)
        short = prob_ref[pair].astype(jnp.bfloat16)
        vgrad[:, at] = dot_nn(short, pair_rows(proj_ref[:, at])).astype(jnp.bfloat16)
    own_ref[...] = vgrad[:own, :]
    frame, member = lax.axis_index("frame"), lax.axis_index("dp")
    inner = HEADS * HEAD_DIM
    share = inner // shares
    pick_row = lax.broadcasted_iota(jnp.int32, (inner, 128), 0)
    pick_col = lax.broadcasted_iota(jnp.int32, (inner, 128), 1)

    def picked(start):
        chosen = (pick_row - pick_col == start) & (pick_col < share)
        pick = jnp.where(chosen, 1.0, 0.0).astype(jnp.bfloat16)
        return dot_nn(vgrad[...], pick).astype(jnp.bfloat16)

    mine_ref[...] = picked((frame * lax.axis_size("dp") + member) * share)
    send_ref[...] = picked((frame * lax.axis_size("dp") + 1 - member) * share)


def backward_kernel(*refs):
    prob_ref, q_ref, k_ref, v_ref, proj_ref, vgrad_ref, upstream_ref, held_ref = refs[:8]
    out_ref, grads = refs[8:]
    count = proj_ref.shape[0]
    own = vgrad_ref.shape[0]
    width = 2 * HEAD_DIM
    lane = lax.broadcasted_iota(jnp.int32, (own, width), 1)
    for pair in range(HEADS // 2):
        at = pl.ds(pair * width, width)
        prob = prob_ref[pair]
        grad_prob = dot_nt(v_ref[:, at], pair_rows(proj_ref[:, at]))
        mean = jnp.sum(grad_prob * prob, axis=0, keepdims=True)
        score_grad = (prob * (grad_prob - mean)).astype(jnp.bfloat16)
        key_grad = dot_nn(score_grad[:own], pair_rows(q_ref[:, at])) * score_scale
        grads[1, :, at] = key_grad.astype(jnp.bfloat16)
        keys = k_ref[:, at]
        first = dot_tn(score_grad[:, :own], keys)
        second = dot_tn(score_grad[:, count : count + own], keys)
        query_grad = jnp.where(lane < HEAD_DIM, first, second) * score_scale
        grads[0, :, at] = query_grad.astype(jnp.bfloat16)
    branch = dot_nt(held_ref[2], vgrad_ref[...])
    branch = branch + dot_nt(held_ref[0], grads[0])
    branch = branch + dot_nt(held_ref[1], grads[1])
    branch = branch.T.astype(jnp.bfloat16).astype(jnp.float32)
    result = upstream_ref[...].astype(jnp.float32) + branch
    out_ref[...] = result.reshape(out_ref.shape).astype(jnp.bfloat16)


def gradient_kernel(row_ref, mine_ref, other_row_ref, other_ref, out_ref):
    total = dot_tn(mine_ref[...], row_ref[...]) + dot_tn(other_ref[...], other_row_ref[...])
    out_ref[...] = total[: out_ref.shape[0]]


VMEM = pl.BlockSpec(memory_space=pltpu.VMEM)
HBM = pl.BlockSpec(memory_space=pltpu.HBM)


def call(kernel, out_shape, in_specs, scratch=(), grant=24):
    return pl.pallas_call(
        kernel,
        out_shape=out_shape,
        in_specs=in_specs,
        out_specs=jax.tree.map(lambda _: VMEM, out_shape),
        scratch_shapes=scratch,
        compiler_params=pltpu.CompilerParams(vmem_limit_bytes=grant * 2**20),
    )


def few_rows_body(acts, cotangent, w_query, w_key, w_value, w_out):
    inputs = acts[0, 0]
    upstream = cotangent[0, 0]
    frames, places, channels = inputs.shape
    inner = w_query.shape[-1]
    count = lax.axis_size("frame")
    shares = count * lax.axis_size("dp")
    own = frames * places
    rows = count * own
    bf16 = jnp.bfloat16
    weights = (w_out[0], w_query[0], w_key[0], w_value[0])
    shape = jax.ShapeDtypeStruct
    turns = range(count - 1, 0, -1)

    def gathered(block):
        received = [block]
        for turn in turns:
            received.append(rotated(block, "frame", turn))
        return received

    blocks = gathered(inputs)
    hbm_args = [pltpu.with_memory_space_constraint(x, pltpu.HBM) for x in (upstream, *weights)]
    projected, upstream_rows, held = call(
        project_kernel,
        (
            shape((own, inner), bf16),
            shape((own, channels), bf16),
            pltpu.VMEM((3, channels, inner), bf16),
        ),
        [HBM] * 5,
        [
            pltpu.VMEM((channels, inner), bf16),
            pltpu.VMEM(upstream.shape, bf16),
            pltpu.SemaphoreType.DMA((5,)),
        ],
    )(*hbm_args)
    all_projected = gathered(projected)
    flat = call(flatten_kernel, shape((rows, channels), bf16), [VMEM] * count)(*blocks)
    other_flat = rotated(flat, "dp", 1)
    wide = shape((rows, inner), bf16)
    queries, key_rows, values, probability = call(
        functools.partial(forward_kernel, places),
        (wide, wide, wide, shape((HEADS // 2, rows, 2 * rows), jnp.float32)),
        [VMEM] * 2,
    )(flat, held)
    narrow = shape((rows, 128), bf16)
    joined, vgrad, mine, send = call(
        functools.partial(value_kernel, count, shares),
        (wide, shape((own, inner), bf16), narrow, narrow),
        [VMEM] * (count + 1),
        [pltpu.VMEM((rows, inner), bf16)],
    )(probability, *all_projected)
    received = rotated(send, "dp", 1)
    result = call(
        backward_kernel,
        shape((frames, places, channels), bf16),
        [VMEM] * 8,
        [pltpu.VMEM((2, own, inner), bf16)],
    )(probability, queries, key_rows, values, joined, vgrad, upstream_rows, held)
    sent_grad = shifted(result, "pipe", -1)
    value_part = call(
        gradient_kernel, shape((inner // shares, channels), jnp.float32), [VMEM] * 4
    )(flat, mine, other_flat, received)
    return (sent_grad[None, None], value_part.T[None])


def few_rows(mesh, acts, inner):
    count, members = mesh.shape["frame"], mesh.shape["dp"]
    rows = acts.shape[2] * acts.shape[3]
    share = inner // (count * members)
    return members == 2 and rows <= 128 and share <= 128 and HEADS % 2 == 0


def solution(mesh):
    specs = (P("pipe", "dp", "frame", None, None),) * 2 + (P("pipe", None, None),) * 4

    def sharded(body):
        return jax.shard_map(
            body,
            mesh=mesh,
            in_specs=specs,
            out_specs=(specs[0], P("pipe", None, ("frame", "dp"))),
            check_vma=False,
        )

    def program(acts, cotangent, *weights):
        if few_rows(mesh, acts, weights[0].shape[-1]):
            return sharded(few_rows_body)(acts, cotangent, *weights)
        return sharded(general_body)(acts, cotangent, *weights)

    return program
```

```python
import functools

import jax
import jax.numpy as jnp
from jax import lax
from jax.experimental import pallas as pl
from jax.experimental.pallas import tpu as pltpu
from jax.sharding import PartitionSpec as P


HEADS = 12
HEAD_DIM = 64


score_scale = 0.125


def shifted(shard, axis, by):
    count = lax.axis_size(axis)
    pairs = [(i, i + by) for i in range(count) if 0 <= i + by < count]
    return lax.ppermute(shard, axis, pairs)


def rotated(shard, axis, by):
    count = lax.axis_size(axis)
    return lax.ppermute(shard, axis, [(i, (i + by) % count) for i in range(count)])


def attend_back(inputs, projected, w_query, w_key, w_value):
    frames = inputs.shape[0]
    places = inputs.shape[1]

    def project_heads(weight):
        result = jnp.dot(inputs, weight, preferred_element_type=jnp.float32).astype(jnp.bfloat16)
        return result.reshape(frames, places, HEADS, HEAD_DIM)

    queries = project_heads(w_query)
    key_rows = project_heads(w_key)
    values = project_heads(w_value)
    scores = (
        jnp.einsum("iphd,jphd->phij", queries, key_rows, preferred_element_type=jnp.float32)
        * score_scale
    )
    probability = jax.nn.softmax(scores, axis=-1)
    prob_short = probability.astype(jnp.bfloat16)
    proj_heads = projected.reshape(frames, places, HEADS, HEAD_DIM)
    grad_prob = jnp.einsum(
        "iphd,jphd->phij", proj_heads, values, preferred_element_type=jnp.float32
    )
    value_grad = jnp.einsum(
        "phij,iphd->jphd", prob_short, proj_heads, preferred_element_type=jnp.float32
    ).astype(jnp.bfloat16)
    score_grad = probability * (
        grad_prob - jnp.sum(grad_prob * probability, axis=-1, keepdims=True)
    )
    score_short = score_grad.astype(jnp.bfloat16)
    query_grad = (
        jnp.einsum("phij,jphd->iphd", score_short, key_rows, preferred_element_type=jnp.float32)
        * score_scale
    ).astype(jnp.bfloat16)
    key_grad = (
        jnp.einsum("phij,iphd->jphd", score_short, queries, preferred_element_type=jnp.float32)
        * score_scale
    ).astype(jnp.bfloat16)
    inner = HEADS * HEAD_DIM
    query_grad = query_grad.reshape(frames, places, inner)
    key_grad = key_grad.reshape(frames, places, inner)
    value_grad = value_grad.reshape(frames, places, inner)
    branch = jnp.einsum("fpj,cj->fpc", query_grad, w_query, preferred_element_type=jnp.float32)
    branch = branch + jnp.einsum("fpj,cj->fpc", key_grad, w_key, preferred_element_type=jnp.float32)
    branch = branch + jnp.einsum(
        "fpj,cj->fpc", value_grad, w_value, preferred_element_type=jnp.float32
    )
    branch = branch.astype(jnp.bfloat16)
    weight_grad = jnp.einsum("fpc,fpj->cj", inputs, value_grad, preferred_element_type=jnp.float32)
    return (branch, weight_grad)


def general_body(acts, cotangent, w_query, w_key, w_value, w_out):
    inputs = acts[0, 0]
    upstream = cotangent[0, 0]
    row_inputs, row_upstream = (
        lax.all_to_all(inputs, "frame", split_axis=1, concat_axis=0, tiled=True),
        lax.all_to_all(upstream, "frame", split_axis=1, concat_axis=0, tiled=True),
    )
    projected = jnp.dot(row_upstream, w_out[0], preferred_element_type=jnp.float32).astype(
        jnp.bfloat16
    )
    branch, value_grad = attend_back(row_inputs, projected, w_query[0], w_key[0], w_value[0])
    row_result = (row_upstream.astype(jnp.float32) + branch.astype(jnp.float32)).astype(
        jnp.bfloat16
    )
    frame_result = lax.all_to_all(row_result, "frame", split_axis=0, concat_axis=1, tiled=True)
    sent_grad = shifted(frame_result[None, None], "pipe", -1)
    value_middle = lax.psum_scatter(
        value_grad.astype(jnp.bfloat16), "frame", scatter_dimension=1, tiled=True
    )
    value_part = lax.psum_scatter(value_middle, "dp", scatter_dimension=1, tiled=True).astype(
        jnp.float32
    )
    return (sent_grad, value_part[None])


def flat_rows(ref):
    block = ref[...]
    frames, places, channels = block.shape
    flat = block.astype(jnp.float32).reshape(frames * places, channels)
    return flat.astype(jnp.bfloat16)


def dot_nn(a, b):
    return jnp.dot(a, b, preferred_element_type=jnp.float32)


def dot_nt(a, b):
    return lax.dot_general(a, b, (((1,), (1,)), ((), ())), preferred_element_type=jnp.float32)


def dot_tn(a, b):
    return lax.dot_general(a, b, (((0,), (0,)), ((), ())), preferred_element_type=jnp.float32)


def tick_kernel(out_ref):
    out_ref[...] = jnp.zeros_like(out_ref)


def project_kernel(upstream_ref, weight_ref, _, out_ref, row_ref):
    rows = flat_rows(upstream_ref)
    row_ref[...] = rows
    out_ref[...] = dot_nn(rows, weight_ref[...]).astype(jnp.bfloat16)


def pair_rows(pair):
    lane = lax.broadcasted_iota(jnp.int32, pair.shape, 1)
    wide = pair.astype(jnp.float32)
    first = jnp.where(lane < HEAD_DIM, wide, 0.0).astype(jnp.bfloat16)
    second = jnp.where(lane < HEAD_DIM, 0.0, wide).astype(jnp.bfloat16)
    return jnp.concatenate([first, second], axis=0)


def flatten_kernel(*refs):
    *act_refs, out_ref = refs
    own = out_ref.shape[0] // len(act_refs)
    for i, ref in enumerate(act_refs):
        out_ref[i * own : (i + 1) * own, :] = flat_rows(ref)


def forward_kernel(places, *refs):
    row_ref, *weight_refs = refs[:4]
    q_ref, k_ref, v_ref, prob_ref = refs[4:]
    rows = row_ref[...]
    for weight_ref, out_ref in zip(weight_refs, (q_ref, k_ref, v_ref)):
        out_ref[...] = dot_nn(rows, weight_ref[...]).astype(jnp.bfloat16)
    count = rows.shape[0]
    row = lax.broadcasted_iota(jnp.int32, (count, 2 * count), 0)
    col = lax.broadcasted_iota(jnp.int32, (count, 2 * count), 1)
    same = lax.rem(row, places) == lax.rem(col, places)
    width = 2 * HEAD_DIM
    for pair in range(HEADS // 2):
        at = pl.ds(pair * width, width)
        scores = dot_nt(k_ref[:, at], pair_rows(q_ref[:, at])) * score_scale
        scores = jnp.where(same, scores, -jnp.inf)
        top = jnp.max(scores, axis=0, keepdims=True)
        raised = jnp.exp(scores - top)
        prob_ref[pair] = raised / jnp.sum(raised, axis=0, keepdims=True)


def value_kernel(blocks, shares, *refs):
    prob_ref, *proj_refs = refs[: blocks + 1]
    proj_ref, own_ref, mine_ref, send_ref, vgrad = refs[blocks + 1 :]
    own = own_ref.shape[0]
    for i, ref in enumerate(proj_refs):
        proj_ref[i * own : (i + 1) * own, :] = ref[...]
    width = 2 * HEAD_DIM
    for pair in range(HEADS // 2):
        at = pl.ds(pair * width, width)
        short = prob_ref[pair].astype(jnp.bfloat16)
        vgrad[:, at] = dot_nn(short, pair_rows(proj_ref[:, at])).astype(jnp.bfloat16)
    own_ref[...] = vgrad[:own, :]
    frame, member = lax.axis_index("frame"), lax.axis_index("dp")
    inner = HEADS * HEAD_DIM
    share = inner // shares
    pick_row = lax.broadcasted_iota(jnp.int32, (inner, 128), 0)
    pick_col = lax.broadcasted_iota(jnp.int32, (inner, 128), 1)

    def picked(start):
        chosen = (pick_row - pick_col == start) & (pick_col < share)
        pick = jnp.where(chosen, 1.0, 0.0).astype(jnp.bfloat16)
        return dot_nn(vgrad[...], pick).astype(jnp.bfloat16)

    mine_ref[...] = picked((frame * lax.axis_size("dp") + member) * share)
    send_ref[...] = picked((frame * lax.axis_size("dp") + 1 - member) * share)


def backward_kernel(*refs):
    prob_ref, q_ref, k_ref, v_ref, proj_ref, vgrad_ref, upstream_ref, *weight_refs = refs[:10]
    out_ref, grads = refs[10:]
    count = proj_ref.shape[0]
    own = vgrad_ref.shape[0]
    width = 2 * HEAD_DIM
    lane = lax.broadcasted_iota(jnp.int32, (own, width), 1)
    for pair in range(HEADS // 2):
        at = pl.ds(pair * width, width)
        prob = prob_ref[pair]
        grad_prob = dot_nt(v_ref[:, at], pair_rows(proj_ref[:, at]))
        mean = jnp.sum(grad_prob * prob, axis=0, keepdims=True)
        score_grad = (prob * (grad_prob - mean)).astype(jnp.bfloat16)
        key_grad = dot_nn(score_grad[:own], pair_rows(q_ref[:, at])) * score_scale
        grads[1, :, at] = key_grad.astype(jnp.bfloat16)
        keys = k_ref[:, at]
        first = dot_tn(score_grad[:, :own], keys)
        second = dot_tn(score_grad[:, count : count + own], keys)
        query_grad = jnp.where(lane < HEAD_DIM, first, second) * score_scale
        grads[0, :, at] = query_grad.astype(jnp.bfloat16)
    branch = dot_nt(weight_refs[2][...], vgrad_ref[...])
    branch = branch + dot_nt(weight_refs[0][...], grads[0])
    branch = branch + dot_nt(weight_refs[1][...], grads[1])
    branch = branch.T.astype(jnp.bfloat16).astype(jnp.float32)
    result = upstream_ref[...].astype(jnp.float32) + branch
    out_ref[...] = result.reshape(out_ref.shape).astype(jnp.bfloat16)


def gradient_kernel(row_ref, mine_ref, other_row_ref, other_ref, out_ref):
    total = dot_tn(mine_ref[...], row_ref[...]) + dot_tn(other_ref[...], other_row_ref[...])
    out_ref[...] = total[: out_ref.shape[0]]


VMEM = pl.BlockSpec(memory_space=pltpu.VMEM)
HBM = pl.BlockSpec(memory_space=pltpu.HBM)


def call(kernel, out_shape, in_specs, scratch=(), flops=0):
    return pl.pallas_call(
        kernel,
        out_shape=out_shape,
        in_specs=in_specs,
        out_specs=jax.tree.map(lambda _: VMEM, out_shape),
        scratch_shapes=scratch,
        compiler_params=pltpu.CompilerParams(vmem_limit_bytes=24 * 2**20),
        cost_estimate=pl.CostEstimate(flops=flops, bytes_accessed=0, transcendentals=0),
    )


def few_rows_body(acts, cotangent, w_query, w_key, w_value, w_out):
    inputs = acts[0, 0]
    upstream = cotangent[0, 0]
    frames, places, channels = inputs.shape
    inner = w_query.shape[-1]
    count = lax.axis_size("frame")
    shares = count * lax.axis_size("dp")
    own = frames * places
    rows = count * own
    bf16 = jnp.bfloat16
    weights = (w_out[0], w_query[0], w_key[0], w_value[0])
    shape = jax.ShapeDtypeStruct
    turns = range(count - 1, 0, -1)

    def gathered(block):
        received = [block]
        for turn in turns:
            received.append(rotated(block, "frame", turn))
        return received

    blocks = gathered(inputs)
    tick = call(tick_kernel, shape((8, 128), jnp.float32), [], flops=4 * 10**10)()
    near = [pltpu.with_memory_space_constraint(x, pltpu.VMEM) for x in (upstream, *weights)]
    projected, upstream_rows = call(
        project_kernel, (shape((own, inner), bf16), shape((own, channels), bf16)), [VMEM] * 3
    )(*near[:2], tick)
    held = near[2:]
    all_projected = gathered(projected)
    flat = call(flatten_kernel, shape((rows, channels), bf16), [VMEM] * count)(*blocks)
    other_flat = rotated(flat, "dp", 1)
    wide = shape((rows, inner), bf16)
    queries, key_rows, values, probability = call(
        functools.partial(forward_kernel, places),
        (wide, wide, wide, shape((HEADS // 2, rows, 2 * rows), jnp.float32)),
        [VMEM] * 4,
    )(flat, *held)
    narrow = shape((rows, 128), bf16)
    joined, vgrad, mine, send = call(
        functools.partial(value_kernel, count, shares),
        (wide, shape((own, inner), bf16), narrow, narrow),
        [VMEM] * (count + 1),
        [pltpu.VMEM((rows, inner), bf16)],
    )(probability, *all_projected)
    received = rotated(send, "dp", 1)
    result = call(
        backward_kernel,
        shape((frames, places, channels), bf16),
        [VMEM] * 10,
        [pltpu.VMEM((2, own, inner), bf16)],
    )(probability, queries, key_rows, values, joined, vgrad, upstream_rows, *held)
    sent_grad = shifted(result[None, None], "pipe", -1)
    value_part = call(
        gradient_kernel, shape((inner // shares, channels), jnp.float32), [VMEM] * 4
    )(flat, mine, other_flat, received)
    return (sent_grad, value_part.T[None])


def few_rows(mesh, acts, inner):
    count, members = mesh.shape["frame"], mesh.shape["dp"]
    rows = acts.shape[2] * acts.shape[3]
    share = inner // (count * members)
    return members == 2 and rows <= 128 and share <= 128 and HEADS % 2 == 0


def solution(mesh):
    specs = (P("pipe", "dp", "frame", None, None),) * 2 + (P("pipe", None, None),) * 4

    def sharded(body):
        return jax.shard_map(
            body,
            mesh=mesh,
            in_specs=specs,
            out_specs=(specs[0], P("pipe", None, ("frame", "dp"))),
            check_vma=False,
        )

    def program(acts, cotangent, *weights):
        if few_rows(mesh, acts, weights[0].shape[-1]):
            return sharded(few_rows_body)(acts, cotangent, *weights)
        return sharded(general_body)(acts, cotangent, *weights)

    return program
```

```python
import functools

import jax
import jax.numpy as jnp
from jax import lax
from jax.experimental import pallas as pl
from jax.experimental.pallas import tpu as pltpu
from jax.sharding import PartitionSpec as P


HEADS = 12
HEAD_DIM = 64


score_scale = 0.125


def shifted(shard, axis, by):
    count = lax.axis_size(axis)
    pairs = [(i, i + by) for i in range(count) if 0 <= i + by < count]
    return lax.ppermute(shard, axis, pairs)


def swapped(shard, axis, by):
    count = lax.axis_size(axis)
    return lax.ppermute(shard, axis, [(i, i ^ by) for i in range(count)])


def rotated(shard, axis, by):
    count = lax.axis_size(axis)
    return lax.ppermute(shard, axis, [(i, (i + by) % count) for i in range(count)])


def partner_order(count):
    return sorted(range(1, count), key=lambda turn: (turn != count // 2, -turn))


def attend_back(inputs, projected, w_query, w_key, w_value):
    frames = inputs.shape[0]
    places = inputs.shape[1]

    def project_heads(weight):
        result = jnp.dot(inputs, weight, preferred_element_type=jnp.float32).astype(jnp.bfloat16)
        return result.reshape(frames, places, HEADS, HEAD_DIM)

    queries = project_heads(w_query)
    key_rows = project_heads(w_key)
    values = project_heads(w_value)
    scores = (
        jnp.einsum("iphd,jphd->phij", queries, key_rows, preferred_element_type=jnp.float32)
        * score_scale
    )
    probability = jax.nn.softmax(scores, axis=-1)
    prob_short = probability.astype(jnp.bfloat16)
    proj_heads = projected.reshape(frames, places, HEADS, HEAD_DIM)
    grad_prob = jnp.einsum(
        "iphd,jphd->phij", proj_heads, values, preferred_element_type=jnp.float32
    )
    value_grad = jnp.einsum(
        "phij,iphd->jphd", prob_short, proj_heads, preferred_element_type=jnp.float32
    ).astype(jnp.bfloat16)
    score_grad = probability * (
        grad_prob - jnp.sum(grad_prob * probability, axis=-1, keepdims=True)
    )
    score_short = score_grad.astype(jnp.bfloat16)
    query_grad = (
        jnp.einsum("phij,jphd->iphd", score_short, key_rows, preferred_element_type=jnp.float32)
        * score_scale
    ).astype(jnp.bfloat16)
    key_grad = (
        jnp.einsum("phij,iphd->jphd", score_short, queries, preferred_element_type=jnp.float32)
        * score_scale
    ).astype(jnp.bfloat16)
    inner = HEADS * HEAD_DIM
    query_grad = query_grad.reshape(frames, places, inner)
    key_grad = key_grad.reshape(frames, places, inner)
    value_grad = value_grad.reshape(frames, places, inner)
    branch = jnp.einsum("fpj,cj->fpc", query_grad, w_query, preferred_element_type=jnp.float32)
    branch = branch + jnp.einsum("fpj,cj->fpc", key_grad, w_key, preferred_element_type=jnp.float32)
    branch = branch + jnp.einsum(
        "fpj,cj->fpc", value_grad, w_value, preferred_element_type=jnp.float32
    )
    branch = branch.astype(jnp.bfloat16)
    weight_grad = jnp.einsum("fpc,fpj->cj", inputs, value_grad, preferred_element_type=jnp.float32)
    return (branch, weight_grad)


def general_body(acts, cotangent, w_query, w_key, w_value, w_out):
    inputs = acts[0, 0]
    upstream = cotangent[0, 0]
    row_inputs, row_upstream = (
        lax.all_to_all(inputs, "frame", split_axis=1, concat_axis=0, tiled=True),
        lax.all_to_all(upstream, "frame", split_axis=1, concat_axis=0, tiled=True),
    )
    projected = jnp.dot(row_upstream, w_out[0], preferred_element_type=jnp.float32).astype(
        jnp.bfloat16
    )
    branch, value_grad = attend_back(row_inputs, projected, w_query[0], w_key[0], w_value[0])
    row_result = (row_upstream.astype(jnp.float32) + branch.astype(jnp.float32)).astype(
        jnp.bfloat16
    )
    frame_result = lax.all_to_all(row_result, "frame", split_axis=0, concat_axis=1, tiled=True)
    sent_grad = shifted(frame_result[None, None], "pipe", -1)
    value_middle = lax.psum_scatter(
        value_grad.astype(jnp.bfloat16), "frame", scatter_dimension=1, tiled=True
    )
    value_part = lax.psum_scatter(value_middle, "dp", scatter_dimension=1, tiled=True).astype(
        jnp.float32
    )
    return (sent_grad, value_part[None])


def flat_rows(ref):
    block = ref[...]
    frames, places, channels = block.shape
    flat = block.astype(jnp.float32).reshape(frames * places, channels)
    return flat.astype(jnp.bfloat16)


def dot_nn(a, b):
    return jnp.dot(a, b, preferred_element_type=jnp.float32)


def dot_nt(a, b):
    return lax.dot_general(a, b, (((1,), (1,)), ((), ())), preferred_element_type=jnp.float32)


def dot_tn(a, b):
    return lax.dot_general(a, b, (((0,), (0,)), ((), ())), preferred_element_type=jnp.float32)


def tick_kernel(out_ref):
    out_ref[...] = jnp.zeros_like(out_ref)


def project_kernel(upstream_ref, weight_ref, _, out_ref, row_ref):
    rows = flat_rows(upstream_ref)
    row_ref[...] = rows
    out_ref[...] = dot_nn(rows, weight_ref[...]).astype(jnp.bfloat16)


def pair_rows(pair):
    lane = lax.broadcasted_iota(jnp.int32, pair.shape, 1)
    wide = pair.astype(jnp.float32)
    first = jnp.where(lane < HEAD_DIM, wide, 0.0).astype(jnp.bfloat16)
    second = jnp.where(lane < HEAD_DIM, 0.0, wide).astype(jnp.bfloat16)
    return jnp.concatenate([first, second], axis=0)


def flatten_kernel(*refs):
    *act_refs, out_ref = refs
    own = out_ref.shape[0] // len(act_refs)
    for i, ref in enumerate(act_refs):
        out_ref[i * own : (i + 1) * own, :] = flat_rows(ref)


def forward_kernel(places, *refs):
    row_ref, *weight_refs = refs[:4]
    q_ref, k_ref, v_ref, prob_ref = refs[4:]
    rows = row_ref[...]
    for weight_ref, out_ref in zip(weight_refs, (q_ref, k_ref, v_ref)):
        out_ref[...] = dot_nn(rows, weight_ref[...]).astype(jnp.bfloat16)
    count = rows.shape[0]
    row = lax.broadcasted_iota(jnp.int32, (count, 2 * count), 0)
    col = lax.broadcasted_iota(jnp.int32, (count, 2 * count), 1)
    same = lax.rem(row, places) == lax.rem(col, places)
    width = 2 * HEAD_DIM
    for pair in range(HEADS // 2):
        at = pl.ds(pair * width, width)
        scores = dot_nt(k_ref[:, at], pair_rows(q_ref[:, at])) * score_scale
        scores = jnp.where(same, scores, -jnp.inf)
        top = jnp.max(scores, axis=0, keepdims=True)
        raised = jnp.exp(scores - top)
        prob_ref[pair] = raised / jnp.sum(raised, axis=0, keepdims=True)


def value_kernel(blocks, shares, *refs):
    prob_ref, *proj_refs = refs[: blocks + 1]
    proj_ref, own_ref, mine_ref, send_ref, vgrad = refs[blocks + 1 :]
    own = own_ref.shape[0]
    for i, ref in enumerate(proj_refs):
        proj_ref[i * own : (i + 1) * own, :] = ref[...]
    width = 2 * HEAD_DIM
    for pair in range(HEADS // 2):
        at = pl.ds(pair * width, width)
        short = prob_ref[pair].astype(jnp.bfloat16)
        vgrad[:, at] = dot_nn(short, pair_rows(proj_ref[:, at])).astype(jnp.bfloat16)
    own_ref[...] = vgrad[:own, :]
    frame, member = lax.axis_index("frame"), lax.axis_index("dp")
    inner = HEADS * HEAD_DIM
    share = inner // shares
    pick_row = lax.broadcasted_iota(jnp.int32, (inner, 128), 0)
    pick_col = lax.broadcasted_iota(jnp.int32, (inner, 128), 1)

    def picked(start):
        chosen = (pick_row - pick_col == start) & (pick_col < share)
        pick = jnp.where(chosen, 1.0, 0.0).astype(jnp.bfloat16)
        return dot_nn(vgrad[...], pick).astype(jnp.bfloat16)

    mine_ref[...] = picked((frame * lax.axis_size("dp") + member) * share)
    send_ref[...] = picked((frame * lax.axis_size("dp") + 1 - member) * share)


def backward_kernel(*refs):
    prob_ref, q_ref, k_ref, v_ref, proj_ref, vgrad_ref, upstream_ref, *weight_refs = refs[:10]
    out_ref, grads = refs[10:]
    count = proj_ref.shape[0]
    own = vgrad_ref.shape[0]
    width = 2 * HEAD_DIM
    lane = lax.broadcasted_iota(jnp.int32, (own, width), 1)
    for pair in range(HEADS // 2):
        at = pl.ds(pair * width, width)
        prob = prob_ref[pair]
        grad_prob = dot_nt(v_ref[:, at], pair_rows(proj_ref[:, at]))
        mean = jnp.sum(grad_prob * prob, axis=0, keepdims=True)
        score_grad = (prob * (grad_prob - mean)).astype(jnp.bfloat16)
        key_grad = dot_nn(score_grad[:own], pair_rows(q_ref[:, at])) * score_scale
        grads[1, :, at] = key_grad.astype(jnp.bfloat16)
        keys = k_ref[:, at]
        first = dot_tn(score_grad[:, :own], keys)
        second = dot_tn(score_grad[:, count : count + own], keys)
        query_grad = jnp.where(lane < HEAD_DIM, first, second) * score_scale
        grads[0, :, at] = query_grad.astype(jnp.bfloat16)
    branch = dot_nt(weight_refs[2][...], vgrad_ref[...])
    branch = branch + dot_nt(weight_refs[0][...], grads[0])
    branch = branch + dot_nt(weight_refs[1][...], grads[1])
    branch = branch.T.astype(jnp.bfloat16).astype(jnp.float32)
    result = upstream_ref[...].astype(jnp.float32) + branch
    out_ref[...] = result.reshape(out_ref.shape).astype(jnp.bfloat16)


def gradient_kernel(row_ref, mine_ref, other_row_ref, other_ref, out_ref):
    total = dot_tn(mine_ref[...], row_ref[...]) + dot_tn(other_ref[...], other_row_ref[...])
    out_ref[...] = total[: out_ref.shape[0]]


VMEM = pl.BlockSpec(memory_space=pltpu.VMEM)
HBM = pl.BlockSpec(memory_space=pltpu.HBM)


def call(kernel, out_shape, in_specs, scratch=(), flops=0):
    return pl.pallas_call(
        kernel,
        out_shape=out_shape,
        in_specs=in_specs,
        out_specs=jax.tree.map(lambda _: VMEM, out_shape),
        scratch_shapes=scratch,
        compiler_params=pltpu.CompilerParams(vmem_limit_bytes=24 * 2**20),
        cost_estimate=pl.CostEstimate(flops=flops, bytes_accessed=0, transcendentals=0),
    )


def few_rows_body(acts, cotangent, w_query, w_key, w_value, w_out):
    inputs = acts[0, 0]
    upstream = cotangent[0, 0]
    frames, places, channels = inputs.shape
    inner = w_query.shape[-1]
    count = lax.axis_size("frame")
    shares = count * lax.axis_size("dp")
    own = frames * places
    rows = count * own
    bf16 = jnp.bfloat16
    weights = (w_out[0], w_query[0], w_key[0], w_value[0])
    shape = jax.ShapeDtypeStruct
    turns = partner_order(count)

    def gathered(block):
        received = [block]
        for turn in turns:
            received.append(swapped(block, "frame", turn))
        return received

    blocks = gathered(inputs)
    tick = call(tick_kernel, shape((8, 128), jnp.float32), [], flops=4 * 10**10)()
    near = [pltpu.with_memory_space_constraint(x, pltpu.VMEM) for x in (upstream, *weights)]
    projected, upstream_rows = call(
        project_kernel, (shape((own, inner), bf16), shape((own, channels), bf16)), [VMEM] * 3
    )(*near[:2], tick)
    held = near[2:]
    all_projected = gathered(projected)
    flat = call(flatten_kernel, shape((rows, channels), bf16), [VMEM] * count)(*blocks)
    other_flat = rotated(flat, "dp", 1)
    wide = shape((rows, inner), bf16)
    queries, key_rows, values, probability = call(
        functools.partial(forward_kernel, places),
        (wide, wide, wide, shape((HEADS // 2, rows, 2 * rows), jnp.float32)),
        [VMEM] * 4,
    )(flat, *held)
    narrow = shape((rows, 128), bf16)
    joined, vgrad, mine, send = call(
        functools.partial(value_kernel, count, shares),
        (wide, shape((own, inner), bf16), narrow, narrow),
        [VMEM] * (count + 1),
        [pltpu.VMEM((rows, inner), bf16)],
    )(probability, *all_projected)
    received = rotated(send, "dp", 1)
    result = call(
        backward_kernel,
        shape((frames, places, channels), bf16),
        [VMEM] * 10,
        [pltpu.VMEM((2, own, inner), bf16)],
    )(probability, queries, key_rows, values, joined, vgrad, upstream_rows, *held)
    sent_grad = rotated(result[None, None], "pipe", -1)
    last = lax.axis_index("pipe") == lax.axis_size("pipe") - 1
    sent_grad = jnp.where(last, jnp.zeros_like(sent_grad), sent_grad)
    value_part = call(
        gradient_kernel, shape((inner // shares, channels), jnp.float32), [VMEM] * 4
    )(flat, mine, other_flat, received)
    return (sent_grad, value_part.T[None])


def few_rows(mesh, acts, inner):
    count, members = mesh.shape["frame"], mesh.shape["dp"]
    rows = acts.shape[2] * acts.shape[3]
    share = inner // (count * members)
    return count & (count - 1) == 0 and members == 2 and rows <= 128 and share <= 128 and HEADS % 2 == 0


def solution(mesh):
    specs = (P("pipe", "dp", "frame", None, None),) * 2 + (P("pipe", None, None),) * 4

    def sharded(body):
        return jax.shard_map(
            body,
            mesh=mesh,
            in_specs=specs,
            out_specs=(specs[0], P("pipe", None, ("frame", "dp"))),
            check_vma=False,
        )

    def program(acts, cotangent, *weights):
        if few_rows(mesh, acts, weights[0].shape[-1]):
            return sharded(few_rows_body)(acts, cotangent, *weights)
        return sharded(general_body)(acts, cotangent, *weights)

    return program
```
